256 devices in a mesh: gx: 8 (over z), gy: 8 (over x, y_hi), gz: 4 (over y_lo, core).
Axes of the slice: x: 4, y: 4 (y_hi: 2, y_lo: 2; y = y_hi * 2 + y_lo), z: 8, core: 2. Of those that a mesh axis runs over, the one named last changes fastest.
Arguments:
- adjoint_in: float32 [14, 128, 128, 512], P(None, 'gx', 'gy', 'gz'), may hold values from -6 to 6
- velocity: float32 [3, 128, 128, 512], P(None, 'gx', 'gy', 'gz'), may hold values from -6 to 6
- viscosity: float32 [128, 128, 512], P('gx', 'gy', 'gz'), may hold values from 0.2 to 2
- rate: float32 [128, 128, 512], P('gx', 'gy', 'gz'), may hold values from 0.1 to 1
- chemistry: float32 [14, 14], replicated, may hold values from -1.5 to 1.5
- stencil_x: float32 [2, 16, 24], replicated, may hold values from -0.875 to 0.875
- stencil_y: float32 [2, 16, 24], replicated, may hold values from -0.875 to 0.875
- stencil_z: float32 [2, 128, 136], replicated, may hold values from -0.375 to 0.375
- sensitivity: float32 [128, 128, 512], P(None, 'gx', 'gz'), may hold values from -0.03125 to 0.03125
- patch_ids: int32 [8, 8, 4], P('gx', 'gy', 'gz'), may hold values from 0 to 255
Outputs:
- adjoint_out: float32 [14, 128, 128, 512], P(None, 'gx', 'gy', 'gz')
- shape_grad: float32 [256, 128], P(('gx', 'gy', 'gz'))
The draws below stay inside these ranges and needn't reach their ends.
All inputs are finite; a program needn't handle non-finite values.
Results may differ from the reference program's by a relative error of at most 0.000078.
Values sent between devices are 32-bit elements; how exact they have to be, the bound alone decides.
No kernel may reach another device: no remote copies, remote signals or barrier semaphores. Data moves between devices by JAX's collectives and lax.ppermute only.
A program may use at most 128 MiB of HBM per device.

```python
import math
import jax
import jax.numpy as jnp
import numpy as np
from jax import lax

NV = 14
NPAR = 128
CX = 16
CY = 16
CZ = 128
NX = 128
NY = 128
NZ = 512
BLOCKS_X = 8
BLOCKS_Y = 8
BLOCKS_Z = 4
NPATCH = 256
N_GX = 8
N_GY = 8
N_GZ = 4


def plant(values, key, least, top_value):
    longest = values.shape.index(max(values.shape))
    spots = []
    for shift in (0, 1):
        where = [jax.random.randint(jax.random.fold_in(key, axis), (), 0, length) for axis, length in enumerate(values.shape)]
        where[longest] = (where[longest] + shift) % values.shape[longest]
        spots.append(tuple(where))
    return values.at[spots[0]].set(least).at[spots[1]].set(top_value)


def block_scale(own_key, extent, shards, low, largest):
    gain = 1.0
    for axis_at, shards_of in shards:
        heights = jax.random.uniform(jax.random.fold_in(jax.random.fold_in(own_key, 6), axis_at), (shards_of,), jnp.float32, low / len(shards), largest / len(shards))
        gain = gain * jnp.repeat(jnp.exp(heights), extent[axis_at] // shards_of).reshape((-1,) + (1,) * (len(extent) - 1 - axis_at))
    return gain


def rank_bounds(count, skew):
    loads = [(1 << 20) // math.isqrt(standing ** skew) + 1 for standing in range(1, count + 1)]
    spread = 1 + sum(loads) // (1 << 30)
    return np.cumsum(np.array([max(1, weight // spread) for weight in loads]))


def ranked_ids(rng, shape, count, skew):
    grid = rank_bounds(count, skew)
    ticket = jax.random.randint(jax.random.fold_in(rng, 1), shape, 0, int(grid[count - 1]))
    grade = jnp.searchsorted(jnp.asarray(grid, jnp.int32), ticket, side="right")
    return jax.random.permutation(jax.random.fold_in(rng, 2), count)[grade].astype(jnp.int32)


def bell_draw(stream_key, dims, scale, bound, pieces=(), held_as=jnp.bfloat16):
    level = block_scale(stream_key, dims, pieces, -0.22, 0.18) if pieces else 1.0
    values = jax.random.normal(stream_key, dims, jnp.float32) * scale * level
    return jnp.minimum(jnp.maximum(values, -bound), bound).astype(held_as)


def setup_inputs(seed: int = 0) -> dict:
    arg_keys = jax.random.split(jax.random.key(seed), 11)
    adjoint_in = bell_draw(arg_keys[0], (NV, NX, NY, NZ), 1.0, 6.0, ((1, 8), (2, 8), (3, 4)), jnp.float32)
    velocity = bell_draw(arg_keys[1], (3, NX, NY, NZ), 1.0, 6.0, ((1, 8), (2, 8), (3, 4)), jnp.float32)
    viscosity = jnp.clip(jnp.exp(math.log(2.0) - 2.3025851 * jax.random.uniform(arg_keys[2], (NX, NY, NZ), jnp.float32) ** block_scale(arg_keys[2], (NX, NY, NZ), ((0, 8), (1, 8), (2, 4)), -0.2, 0.2)), 0.2, 2.0)
    rate = jnp.clip(jnp.exp(math.log(1.0) - 2.3025851 * jax.random.uniform(arg_keys[3], (NX, NY, NZ), jnp.float32) ** block_scale(arg_keys[3], (NX, NY, NZ), ((0, 8), (1, 8), (2, 4)), -0.2, 0.2)), 0.1, 1.0)
    chemistry = bell_draw(arg_keys[4], (NV, NV), NV ** -0.5, 1.5, (), jnp.float32)
    stencil_x = bell_draw(arg_keys[5], (2, CX, CX + 8), (2 * (CX + 8)) ** -0.5, 0.875, (), jnp.float32)
    stencil_y = bell_draw(arg_keys[6], (2, CY, CY + 8), (2 * (CY + 8)) ** -0.5, 0.875, (), jnp.float32)
    stencil_z = bell_draw(arg_keys[7], (2, CZ, CZ + 8), (2 * (CZ + 8)) ** -0.5, 0.375, (), jnp.float32)
    sensitivity = bell_draw(arg_keys[8], (NPAR, NX, NZ), (CX * CY * CZ) ** -0.5, 0.03125, ((1, 8), (2, 4)), jnp.float32)
    patch_ids = plant(ranked_ids(arg_keys[9], (BLOCKS_X, BLOCKS_Y, BLOCKS_Z), NPATCH, 2), jax.random.fold_in(arg_keys[9], 3), 0, NPATCH - 1).astype(jnp.int32)
    return dict(adjoint_in=adjoint_in, velocity=velocity, viscosity=viscosity, rate=rate, chemistry=chemistry, stencil_x=stencil_x, stencil_y=stencil_y, stencil_z=stencil_z, sensitivity=sensitivity, patch_ids=patch_ids)


section_step = 0.5
hydrogen = 5
highest = lax.Precision.HIGHEST


def blocked(grid_field, along_axis, num_blocks, block_len, stencil):
    pad_widths = [(0, 0), (0, 0), (0, 0)]
    pad_widths[along_axis] = (4, 4)
    padded = jnp.pad(grid_field, pad_widths)
    positions = (jnp.arange(num_blocks)[:, None] * block_len + jnp.arange(block_len + 8)[None, :]).reshape(-1).astype(jnp.int32)
    window = jnp.take(padded, positions, axis=along_axis)
    window = jnp.moveaxis(window, along_axis, -1)
    lead_shape = window.shape[:-1]
    window = window.reshape(lead_shape + (num_blocks, block_len + 8))
    result = jnp.dot(window, stencil.T, precision=highest)
    result = result.reshape(lead_shape + (num_blocks * block_len,))
    return jnp.moveaxis(result, -1, along_axis)


def direction_term(adjoint_comp, advect, viscosity, along_axis, num_blocks, block_len, stencil):
    first = blocked(-advect * adjoint_comp, along_axis, num_blocks, block_len, stencil[0])
    second = blocked(viscosity * adjoint_comp, along_axis, num_blocks, block_len, stencil[1])
    return first + second


def reference(adjoint_in, velocity, viscosity, rate, chemistry, stencil_x, stencil_y, stencil_z, sensitivity, patch_ids):
    def per_component(adjoint_comp):
        total = direction_term(adjoint_comp, velocity[0], viscosity, 0, N_GX, CX, stencil_x)
        total = total + direction_term(adjoint_comp, velocity[1], viscosity, 1, N_GY, CY, stencil_y)
        total = total + direction_term(adjoint_comp, velocity[2], viscosity, 2, N_GZ, CZ, stencil_z)
        return total

    transport = lax.map(per_component, adjoint_in)
    reacting = jnp.tensordot(chemistry.T, rate[None] * adjoint_in, axes=1, precision=highest)
    adjoint_out = adjoint_in + section_step * (transport + reacting)
    blocks_hyd = adjoint_in[hydrogen].reshape(N_GX, CX, N_GY, CY, N_GZ, CZ)
    sens_blocks = sensitivity.reshape(NPAR, N_GX, CX, N_GZ, CZ)
    partials = jnp.einsum("aibjck,paick->abcp", blocks_hyd, sens_blocks, precision=highest).reshape(-1, NPAR)
    owners = patch_ids.reshape(-1).astype(jnp.int32)
    selector = (owners[:, None] == jnp.arange(NPATCH, dtype=jnp.int32)[None, :]).astype(jnp.float32)
    shape_grad = section_step * jnp.dot(selector.T, partials, precision=highest)
    return adjoint_out, shape_grad
```

```python
import functools

import jax
import jax.numpy as jnp
from jax import lax
from jax.experimental import pallas as pl
from jax.experimental.pallas import tpu as pltpu
from jax.sharding import PartitionSpec as P

section_step = 0.5
hydrogen = 5
highest = lax.Precision.HIGHEST
AXES = ("gx", "gy", "gz")
f32, bf16, i32 = jnp.float32, jnp.bfloat16, jnp.int32


def swap(a, b, axis):
    n = lax.axis_size(axis)
    plan_a = [(i, i ^ 1) for i in range(n)]
    plan_b = [(i, (i - 1) % n if i % 2 == 0 else (i + 1) % n) for i in range(n)]
    return lax.ppermute(a, axis, plan_a), lax.ppermute(b, axis, plan_b)


def is_even(axis):
    return lax.rem(lax.axis_index(axis), 2) == 0


def iota(shape, dim):
    return lax.broadcasted_iota(i32, shape, dim)


def split(x):
    hi = x.astype(bf16)
    return hi, (x - hi.astype(f32)).astype(bf16)


def mm(a, b):
    return jnp.dot(a, b, preferred_element_type=f32)


CHUNKS = ((0, 4), (4, 8), (8, 12), (12, 16))


def pack_xy(adj, vel, visc, gya, gyb, gxa, gxb, buf, oa, ob, sem_in, sem_x, sem_out):
    nv = adj.shape[0]
    even_x, even_y = is_even("gx"), is_even("gy")
    ins = []
    for k, (c0, c1) in enumerate(CHUNKS):
        top = min(c1, nv)
        group = [pltpu.make_async_copy(adj.at[c0:top], buf.at[c0:top], sem_in.at[k, 0])]
        if c1 > nv:
            group.append(pltpu.make_async_copy(vel.at[1], buf.at[nv], sem_in.at[k, 1]))
            group.append(pltpu.make_async_copy(visc, buf.at[nv + 1], sem_in.at[k, 2]))
        for c in group:
            c.start()
        ins.append(group)
    xs = []
    last = adj.shape[1] - 4
    for side, out in enumerate((gxa, gxb)):
        want_last = even_x if side == 0 else jnp.logical_not(even_x)
        at = pl.ds(jnp.where(want_last, last, 0), 4)
        xs.append(pltpu.make_async_copy(adj.at[:, at], out.at[0:nv], sem_x.at[side, 0]))
        xs.append(pltpu.make_async_copy(vel.at[0, at], out.at[nv], sem_x.at[side, 1]))
        xs.append(pltpu.make_async_copy(visc.at[at], out.at[nv + 1], sem_x.at[side, 2]))
    for c in xs:
        c.start()
    outs = []
    for k, (c0, c1) in enumerate(CHUNKS):
        for c in ins[k]:
            c.wait()
        first = jnp.concatenate([buf[c0:c1, 8:16, 0:4, :], buf[c0:c1, 0:8, 0:4, :]], axis=2)
        final = jnp.concatenate([buf[c0:c1, 8:16, 12:16, :], buf[c0:c1, 0:8, 12:16, :]], axis=2)
        oa[c0:c1] = jnp.where(even_y, final, first)
        ob[c0:c1] = jnp.where(even_y, first, final)
        for side, (src, dst) in enumerate(((oa, gya), (ob, gyb))):
            c = pltpu.make_async_copy(src.at[c0:c1], dst.at[c0:c1], sem_out.at[side, k])
            c.start()
            outs.append(c)
    for c in xs + outs:
        c.wait()


def call_pack_xy(adj, vel, visc):
    nv = adj.shape[0]
    gy = jax.ShapeDtypeStruct((nv + 2, 8, 8, 128), f32)
    gx = jax.ShapeDtypeStruct((nv + 2, 4, 16, 128), f32)
    anyspec = pl.BlockSpec(memory_space=pl.ANY)
    return pl.pallas_call(
        pack_xy,
        out_shape=(gy, gy, gx, gx),
        in_specs=[anyspec] * 3,
        out_specs=(anyspec,) * 4,
        scratch_shapes=[
            pltpu.VMEM((nv + 2, 16, 16, 128), f32),
            pltpu.VMEM((nv + 2, 8, 8, 128), f32),
            pltpu.VMEM((nv + 2, 8, 8, 128), f32),
            pltpu.SemaphoreType.DMA((4, 3)),
            pltpu.SemaphoreType.DMA((2, 3)),
            pltpu.SemaphoreType.DMA((2, 4)),
        ],
        compiler_params=pltpu.CompilerParams(vmem_limit_bytes=24 << 20),
        cost_estimate=pl.CostEstimate(flops=0, bytes_accessed=6 << 20, transcendentals=0),
        name="pack_xy",
    )(adj, vel, visc)


def pack_z(ids, adj, vel, visc, sens, gza, gzb, contrib):
    nv = adj.shape[0]
    lane = iota((256, 128), 1)
    face = jnp.zeros((256, 128), f32)
    for c in range(nv + 2):
        field = adj[c] if c < nv else (vel[0] if c == nv else visc[...])
        face = jnp.where(lane >> 3 == c, pltpu.roll(field, (8 * c + 4) % 128, 1), face)
    low = (iota((128, 128), 1) & 4) == 0
    top, bottom = face[:128], face[128:]
    finals = jnp.where(low, top, pltpu.roll(bottom, 4, 1))
    firsts = jnp.where(low, pltpu.roll(top, 124, 1), bottom)
    even = is_even("gz")
    gza[...] = jnp.where(even, finals, firsts)
    gzb[...] = jnp.where(even, firsts, finals)
    column = jnp.sum(adj[hydrogen].reshape(16, 16, 128), axis=1)
    terms = jnp.sum(sens[...] * column[None], axis=1)
    partial = jnp.sum(terms.T, axis=0, keepdims=True)
    owner = iota(contrib.shape, 0) == ids[0]
    contrib[...] = jnp.where(owner, jnp.broadcast_to(partial, contrib.shape), 0.0)


def call_pack_z(ids, adj, vel, visc, sens, patches):
    nv = adj.shape[0]
    face = jax.ShapeDtypeStruct((128, 128), f32)
    vm = pl.BlockSpec(memory_space=pltpu.VMEM)
    return pl.pallas_call(
        pack_z,
        grid=(1,),
        out_shape=(face, face, jax.ShapeDtypeStruct((patches, 128), f32)),
        in_specs=[
            pl.BlockSpec(memory_space=pltpu.SMEM),
            pl.BlockSpec((nv, 256, 128), lambda i: (0, 0, 0)),
            pl.BlockSpec((1, 256, 128), lambda i: (2, 0, 0)),
            vm,
            vm,
        ],
        out_specs=(vm, vm, vm),
        compiler_params=pltpu.CompilerParams(vmem_limit_bytes=24 << 20),
        cost_estimate=pl.CostEstimate(flops=1 << 20, bytes_accessed=4 << 20, transcendentals=0),
        name="pack_z",
    )(ids, adj, vel, visc, sens)


def halo_columns(axis, in_a, j, length):
    index, n = lax.axis_index(axis), lax.axis_size(axis)
    even = is_even(axis)
    after = jnp.where(even, in_a, 1 - in_a) == 1
    col = jnp.where(after, length + 4 + j, j)
    has_after = jnp.where(index < n - 1, 1, 0)
    has_before = jnp.where(index > 0, 1, 0)
    return jnp.where(jnp.where(after, has_after, has_before) == 1, col, -1)


def build_matrices(sx, sy, m_loc, m_halo_hi, m_halo_lo):
    rows, k16 = iota((256, 16), 0), iota((256, 16), 1)
    pick_x = (rows >> 4 == k16).astype(f32)
    pick_y = (rows & 15 == k16).astype(f32)
    c_loc, k_loc = iota((24, 256), 1), iota((24, 256), 0)
    c_halo, k_halo = iota((24, 128), 1), iota((24, 128), 0)
    in_a = jnp.where(c_halo < 64, 1, 0)
    col_x = halo_columns("gx", in_a, (c_halo & 63) >> 4, 16)
    col_y = halo_columns("gy", in_a, c_halo & 3, 16)
    cols_x = jnp.concatenate([k_loc == 4 + (c_loc >> 4), k_halo == col_x], axis=1).astype(f32)
    cols_y = jnp.concatenate([k_loc == 4 + (c_loc & 15), k_halo == col_y], axis=1).astype(f32)
    dot = functools.partial(jnp.dot, precision=highest, preferred_element_type=f32)
    r, c = iota((256, 256), 0), iota((256, 256), 1)
    same_y, same_x = (r & 15) == (c & 15), (r >> 4) == (c >> 4)
    rh, ch = iota((256, 128), 0), iota((256, 128), 1)
    same_yh = (rh & 15) == (ch & 15)
    x_of = ((ch & 63) >> 3) + jnp.where((ch & 7) >= 4, 0, 8)
    same_xh = (rh >> 4) == x_of
    full = []
    for f, scale in ((0, -section_step), (1, section_step)):
        tx = dot(dot(pick_x, sx[f] * scale), cols_x)
        ty = dot(dot(pick_y, sy[f] * scale), cols_y)
        full.append((jnp.where(same_y, tx[:, :256], 0.0), jnp.where(same_x, ty[:, :256], 0.0)))
        for part, (mask, t) in enumerate(((same_yh, tx), (same_xh, ty))):
            hi, lo = split(jnp.where(mask, t[:, 256:], 0.0))
            at = (2 * part + f) * 128
            m_halo_hi[:, at : at + 128] = hi
            m_halo_lo[:, at : at + 128] = lo
    for g, m in enumerate((full[0][0], full[0][1], full[1][0] + full[1][1])):
        hi, lo = split(m)
        m_loc[:, g * 256 : g * 256 + 256] = hi
        m_loc[:, 768 + g * 256 : 768 + g * 256 + 256] = lo


def interior(
    chem, adj, vel, visc, rate, sx, sy, szt, out, m_halo_hi, m_halo_lo, tile_hi, tile_lo, m_loc, wz
):
    nv = adj.shape[0]
    build_matrices(sx, sy, m_loc, m_halo_hi, m_halo_lo)
    index, n = lax.axis_index("gz"), lax.axis_size("gz")
    before = jnp.where(index > 0, 1.0, 0.0)
    after = jnp.where(index < n - 1, 1.0, 0.0)
    for f, scale in ((0, -section_step), (1, section_step)):
        hi, lo = split(szt[f, 4:132, :] * scale)
        wz[f * 128 : f * 128 + 128, 0:128] = hi
        wz[f * 128 : f * 128 + 128, 128:256] = lo
        ends = jnp.concatenate(
            [szt[f, 0:4, :] * (scale * before), szt[f, 132:136, :] * (scale * after)], axis=0
        )
        hi, lo = split(jnp.concatenate([ends] * 16, axis=0))
        tile_hi[f * 128 : f * 128 + 128, :] = hi
        tile_lo[f * 128 : f * 128 + 128, :] = lo

    def pair(i, carry):
        highs, lows, zs = [], [], []
        for k in range(2):
            a = adj[2 * i + k]
            parts = [split(vel[0] * a), split(vel[1] * a), split(visc[...] * a)]
            highs.append(jnp.concatenate([p[0] for p in parts], axis=0))
            lows.append(jnp.concatenate([p[1] for p in parts], axis=0))
            z = split(vel[2] * a)
            z_hi = jnp.concatenate([z[0], parts[2][0]], axis=1)
            z_lo = jnp.concatenate([z[1], parts[2][1]], axis=1)
            both = mm(z_hi, wz[...])
            zs.append(both[:, :128] + both[:, 128:] + mm(z_lo, wz[:, :128]))
        hi, lo = jnp.concatenate(highs, axis=1), jnp.concatenate(lows, axis=1)
        xy = mm(m_loc[:, :768], hi) + mm(m_loc[:, :768], lo) + mm(m_loc[:, 768:], hi)
        for k in range(2):
            v = 2 * i + k
            total = adj[v] + xy[:, k * 128 : k * 128 + 128] + zs[k]
            mixed = (chem[0, v] * section_step) * adj[0]
            for u in range(1, nv):
                mixed = mixed + (chem[u, v] * section_step) * adj[u]
            out[v] = total + rate[...] * mixed
        return carry

    lax.fori_loop(0, nv // 2, pair, 0)


def call_interior(chem, adj, vel, visc, rate, sx, sy, szt):
    nv = adj.shape[0]
    vm = pl.BlockSpec(memory_space=pltpu.VMEM)
    return pl.pallas_call(
        interior,
        out_shape=(
            jax.ShapeDtypeStruct((nv, 256, 128), f32),
            jax.ShapeDtypeStruct((256, 512), bf16),
            jax.ShapeDtypeStruct((256, 512), bf16),
            jax.ShapeDtypeStruct((256, 128), bf16),
            jax.ShapeDtypeStruct((256, 128), bf16),
        ),
        in_specs=[pl.BlockSpec(memory_space=pltpu.SMEM)] + [vm] * 7,
        out_specs=(vm,) * 5,
        scratch_shapes=[pltpu.VMEM((256, 1536), bf16), pltpu.VMEM((256, 256), bf16)],
        compiler_params=pltpu.CompilerParams(vmem_limit_bytes=32 << 20),
        cost_estimate=pl.CostEstimate(flops=4 << 30, bytes_accessed=6 << 20, transcendentals=0),
        name="interior",
    )(chem, adj, vel, visc, rate, sx, sy, szt)


def spread(face, lane, group):
    x = jnp.where(lane >> 3 == group, face, 0.0)
    for shift in (64, 32, 16, 8):
        x = x + pltpu.roll(x, shift, 1)
    return x


def finish(base, gxa, gxb, gya, gyb, gza, gzb, m_hi, m_lo, tile_hi, tile_lo, rows, out, grad):
    nv = base.shape[0]
    grad[...] = section_step * jnp.sum(rows[...], axis=0, keepdims=True)
    even = is_even("gz")
    before = jnp.where(even, gzb[...], gza[...])
    after = jnp.where(even, gza[...], gzb[...])
    low = (iota((128, 128), 1) & 4) == 0
    face = jnp.concatenate(
        [
            jnp.where(low, before, pltpu.roll(after, 4, 1)),
            jnp.where(low, pltpu.roll(before, 124, 1), after),
        ],
        axis=0,
    )
    lane = iota((256, 128), 1)
    z_hi, z_lo = split(
        jnp.concatenate([spread(face, lane, nv) * face, spread(face, lane, nv + 1) * face], axis=1)
    )
    group = (iota((256, 128), 0) & 127) >> 3

    def pair(i, carry):
        highs, lows, w_his, w_los = [], [], [], []
        for k in range(2):
            v = 2 * i + k
            parts = []
            for a, b in ((gxa, gxb), (gya, gyb)):
                for f in (nv, nv + 1):
                    parts.append(a[v] * a[f])
                    parts.append(b[v] * b[f])
            hi, lo = split(jnp.concatenate(parts, axis=0))
            highs.append(hi)
            lows.append(lo)
            w_his.append(jnp.where(group == v, tile_hi[...].astype(f32), 0.0).astype(bf16))
            w_los.append(jnp.where(group == v, tile_lo[...].astype(f32), 0.0).astype(bf16))
        hi, lo = jnp.concatenate(highs, axis=1), jnp.concatenate(lows, axis=1)
        w_hi, w_lo = jnp.concatenate(w_his, axis=1), jnp.concatenate(w_los, axis=1)
        t = mm(m_hi[...], hi) + mm(m_hi[...], lo) + mm(m_lo[...], hi)
        t = t + mm(z_hi, w_hi) + mm(z_lo, w_hi) + mm(z_hi, w_lo)
        for k in range(2):
            out[2 * i + k] = base[2 * i + k] + t[:, k * 128 : k * 128 + 128]
        return carry

    lax.fori_loop(0, nv // 2, pair, 0)


def call_finish(base, faces, mats, rows):
    nv = base.shape[0]
    vm = pl.BlockSpec(memory_space=pltpu.VMEM)
    return pl.pallas_call(
        finish,
        out_shape=(
            jax.ShapeDtypeStruct((nv, 256, 128), f32),
            jax.ShapeDtypeStruct((1, 128), f32),
        ),
        in_specs=[vm] * 12,
        out_specs=(vm, vm),
        compiler_params=pltpu.CompilerParams(vmem_limit_bytes=32 << 20),
        cost_estimate=pl.CostEstimate(flops=2 << 30, bytes_accessed=8 << 20, transcendentals=0),
        name="finish",
    )(base, *faces, *mats, rows)


def shards(
    adjoint_in,
    velocity,
    viscosity,
    rate,
    chemistry,
    stencil_x,
    stencil_y,
    stencil_z,
    sensitivity,
    patch_ids,
):
    nv = adjoint_in.shape[0]
    assert adjoint_in.shape[1:] == (16, 16, 128) and nv == 14 and sensitivity.shape[0] == 128
    devices = lax.axis_size("gx") * lax.axis_size("gy") * lax.axis_size("gz")
    gya, gyb, gxa, gxb = call_pack_xy(adjoint_in, velocity, viscosity)
    gya, gyb = swap(gya, gyb, "gy")
    gxa, gxb = swap(gxa, gxb, "gx")
    adj = adjoint_in.reshape(nv, 256, 128)
    vel = velocity.reshape(3, 256, 128)
    visc = viscosity.reshape(256, 128)
    gza, gzb, contrib = call_pack_z(patch_ids.reshape(1), adj, vel, visc, sensitivity, devices)
    gza, gzb = swap(gza, gzb, "gz")
    rows = lax.all_to_all(contrib, AXES, 0, 0, tiled=True)
    base, *mats = call_interior(
        chemistry, adj, vel, visc, rate.reshape(256, 128), stencil_x, stencil_y,
        jnp.swapaxes(stencil_z, 1, 2),
    )
    flat = lambda x: x.reshape(nv + 2, 64, 128)
    faces = (flat(gxa), flat(gxb), flat(gya), flat(gyb), gza, gzb)
    out, grad = call_finish(base, faces, mats, rows)
    return out.reshape(adjoint_in.shape), grad


def solution(mesh):
    return jax.shard_map(
        shards,
        mesh=mesh,
        in_specs=(
            P(None, "gx", "gy", "gz"),
            P(None, "gx", "gy", "gz"),
            P("gx", "gy", "gz"),
            P("gx", "gy", "gz"),
            P(),
            P(),
            P(),
            P(),
            P(None, "gx", "gz"),
            P("gx", "gy", "gz"),
        ),
        out_specs=(P(None, "gx", "gy", "gz"), P(("gx", "gy", "gz"), None)),
        check_vma=False,
    )
```

```python
import functools

import jax
import jax.numpy as jnp
from jax import lax
from jax.experimental import pallas as pl
from jax.experimental.pallas import tpu as pltpu
from jax.sharding import PartitionSpec as P

section_step = 0.5
hydrogen = 5
AXES = ("gx", "gy", "gz")
f32, bf16, i32 = jnp.float32, jnp.bfloat16, jnp.int32


def swap(a, b, axis):
    n = lax.axis_size(axis)
    plan_a = [(i, i ^ 1) for i in range(n)]
    plan_b = [(i, (i - 1) % n if i % 2 == 0 else (i + 1) % n) for i in range(n)]
    return lax.ppermute(a, axis, plan_a), lax.ppermute(b, axis, plan_b)


def is_even(axis):
    return lax.rem(lax.axis_index(axis), 2) == 0


def iota(shape, dim):
    return lax.broadcasted_iota(i32, shape, dim)


def split(x):
    hi = x.astype(bf16)
    return hi, (x - hi.astype(f32)).astype(bf16)


def mm(a, b):
    return jnp.dot(a, b, preferred_element_type=f32)


hbm = pl.BlockSpec(memory_space=pl.ANY)
vm = pl.BlockSpec(memory_space=pltpu.VMEM)


def params(mib):
    return pltpu.CompilerParams(vmem_limit_bytes=mib << 20)


def cost(flops, mib):
    return pl.CostEstimate(flops=1, bytes_accessed=1024, transcendentals=0)


def in_hbm(x):
    return pltpu.with_memory_space_constraint(x, pltpu.HBM)


def in_vmem(x):
    return pltpu.with_memory_space_constraint(x, pltpu.VMEM)


def resident(*shape, dtype=f32):
    return pltpu.VMEM(shape, dtype)


CHUNKS = ((0, 4), (4, 8), (8, 12), (12, 16))


def pack_y(adj, vel, visc, gya, gyb, fields, oa, ob, sem_in, sem_out):
    nv = adj.shape[0]
    ins = []
    for k, (c0, c1) in enumerate(CHUNKS):
        top = min(c1, nv)
        group = [pltpu.make_async_copy(adj.at[c0:top], fields.at[c0:top], sem_in.at[k, 0])]
        if c1 > nv:
            group.append(pltpu.make_async_copy(vel.at[1], fields.at[nv], sem_in.at[k, 1]))
            group.append(pltpu.make_async_copy(visc, fields.at[nv + 1], sem_in.at[k, 2]))
        for c in group:
            c.start()
        ins.append(group)
    even = is_even("gy")
    outs = []
    for k, (c0, c1) in enumerate(CHUNKS):
        for c in ins[k]:
            c.wait()
        for c in range(c0, c1):
            x = fields[c].reshape(16, 16, 128)
            first = jnp.concatenate([x[8:16, 0:4, :], x[0:8, 0:4, :]], axis=1).reshape(64, 128)
            final = jnp.concatenate([x[8:16, 12:16, :], x[0:8, 12:16, :]], axis=1).reshape(64, 128)
            oa[c] = jnp.where(even, final, first)
            ob[c] = jnp.where(even, first, final)
        for side, (src, dst) in enumerate(((oa, gya), (ob, gyb))):
            c = pltpu.make_async_copy(src.at[c0:c1], dst.at[c0:c1], sem_out.at[side, k])
            c.start()
            outs.append(c)
    for c in outs:
        c.wait()


def call_pack_y(adj, vel, visc):
    nv = adj.shape[0]
    gy = pltpu.HBM((nv + 2, 64, 128), f32)
    return pl.pallas_call(
        pack_y,
        out_shape=(gy, gy, resident(nv + 2, 256, 128)),
        in_specs=[hbm] * 3,
        out_specs=(hbm, hbm, vm),
        scratch_shapes=[
            pltpu.VMEM((nv + 2, 64, 128), f32),
            pltpu.VMEM((nv + 2, 64, 128), f32),
            pltpu.SemaphoreType.DMA((4, 3)),
            pltpu.SemaphoreType.DMA((2, 4)),
        ],
        compiler_params=params(16),
        cost_estimate=cost(0, 4),
        name="pack_y",
    )(in_hbm(adj), in_hbm(vel), in_hbm(visc))


def pack_xz(
    ids, fields, vel, sens, gxa, gxb, gza, gzb, contrib,
    more, zbuf, sens_buf, sem_in, sem_x, sem_z, sem_s,
):
    channels = fields.shape[0]
    nv = channels - 2
    ins = [
        pltpu.make_async_copy(src, more.at[k], sem_in.at[k])
        for k, src in enumerate((vel.at[0], vel.at[2]))
    ]
    load_sens = pltpu.make_async_copy(sens, sens_buf, sem_s)
    for c in ins + [load_sens]:
        c.start()
    want_last = is_even("gx")
    xs = []
    for side, out in enumerate((gxa, gxb)):
        take_last = want_last if side == 0 else jnp.logical_not(want_last)
        at = pl.ds(pl.multiple_of(jnp.where(take_last, 192, 0), 64), 64)
        xs.append(pltpu.make_async_copy(fields.at[0:nv, at], out.at[0:nv], sem_x.at[side, 0]))
        xs.append(pltpu.make_async_copy(fields.at[nv + 1, at], out.at[nv + 1], sem_x.at[side, 1]))
        xs.append(pltpu.make_async_copy(more.at[0, at], out.at[nv], sem_x.at[side, 2]))
        xs[-3].start()
        xs[-2].start()
    ins[0].wait()
    xs[2].start()
    xs[5].start()
    lane = iota((256, 128), 1)
    face = jnp.zeros((256, 128), f32)
    ins[1].wait()
    for c in range(channels):
        field = more[1] if c == nv else fields[c]
        face = jnp.where(lane >> 3 == c, pltpu.roll(field, (8 * c + 4) % 128, 1), face)
    low = (iota((128, 128), 1) & 4) == 0
    top, bottom = face[:128], face[128:]
    finals = jnp.where(low, top, pltpu.roll(bottom, 4, 1))
    firsts = jnp.where(low, pltpu.roll(top, 124, 1), bottom)
    even = is_even("gz")
    zbuf[0] = jnp.where(even, finals, firsts)
    zbuf[1] = jnp.where(even, firsts, finals)
    for side, dst in enumerate((gza, gzb)):
        xs.append(pltpu.make_async_copy(zbuf.at[side], dst, sem_z.at[side]))
        xs[-1].start()
    column = jnp.sum(fields[hydrogen].reshape(16, 16, 128), axis=1)
    load_sens.wait()
    terms = jnp.sum(sens_buf[...] * column[None], axis=1)
    partial = jnp.sum(terms.T, axis=0, keepdims=True)
    owner = iota(contrib.shape, 0) == jnp.broadcast_to(ids[0], contrib.shape)
    contrib[...] = jnp.where(owner, jnp.broadcast_to(partial, contrib.shape), 0.0)
    for c in xs:
        c.wait()


def call_pack_xz(ids, fields, vel, sens, patches):
    channels = fields.shape[0]
    gx = pltpu.HBM((channels, 64, 128), f32)
    gz = pltpu.HBM((128, 128), f32)
    return pl.pallas_call(
        pack_xz,
        out_shape=(gx, gx, gz, gz, jax.ShapeDtypeStruct((patches, 128), f32)),
        in_specs=[vm, vm] + [hbm] * 2,
        out_specs=(hbm, hbm, hbm, hbm, vm),
        scratch_shapes=[
            pltpu.VMEM((2, 256, 128), f32),
            pltpu.VMEM((2, 128, 128), f32),
            pltpu.VMEM(sens.shape, f32),
            pltpu.SemaphoreType.DMA((2,)),
            pltpu.SemaphoreType.DMA((2, 3)),
            pltpu.SemaphoreType.DMA((2,)),
            pltpu.SemaphoreType.DMA,
        ],
        compiler_params=params(16),
        cost_estimate=cost(1 << 20, 6),
        name="pack_xz",
    )(ids, fields, vel, sens)


def halo_columns(axis, in_a, j, length):
    index, n = lax.axis_index(axis), lax.axis_size(axis)
    even = is_even(axis)
    after = jnp.where(even, in_a, 1 - in_a) == 1
    col = jnp.where(after, length + 4 + j, j)
    has_after = jnp.where(index < n - 1, 1, 0)
    has_before = jnp.where(index > 0, 1, 0)
    return jnp.where(jnp.where(after, has_after, has_before) == 1, col, -1)


WIDE = 3 * 256
EDGE = 4 * 128


def expand(s, cols):
    halves = [split(s[0] * -section_step), split(s[1] * section_step)]
    pieces = mm(jnp.concatenate([h for pair in halves for h in pair], axis=0), cols)
    return [pieces[32 * f : 32 * f + 16] + pieces[32 * f + 16 : 32 * f + 32] for f in range(2)]


def per_x(piece):
    shape = (16, 16, piece.shape[1])
    return jnp.broadcast_to(piece[:, None, :], shape).reshape(256, shape[2])


def per_y(piece):
    shape = (16, 16, piece.shape[1])
    return jnp.broadcast_to(piece[None], shape).reshape(256, shape[2])


def store_thrice(ref, blocks):
    wide, at = ref.shape[1] // 3, 0
    for block in blocks:
        hi, lo = split(block)
        n = block.shape[1]
        ref[:, at : at + n] = hi
        ref[:, wide + at : wide + at + n] = hi
        ref[:, 2 * wide + at : 2 * wide + at + n] = lo
        at += n


def build_matrices(sx, sy, matrix, edge):
    c_loc, k_loc = iota((24, 256), 1), iota((24, 256), 0)
    c_halo, k_halo = iota((24, 128), 1), iota((24, 128), 0)
    in_a = jnp.where(c_halo < 64, 1, 0)
    col_x = halo_columns("gx", in_a, (c_halo & 63) >> 4, 16)
    col_y = halo_columns("gy", in_a, c_halo & 3, 16)
    hot = lambda x: jnp.where(x, 1.0, 0.0)
    cols_x = jnp.concatenate([hot(k_loc == 4 + (c_loc >> 4)), hot(k_halo == col_x)], axis=1)
    cols_y = jnp.concatenate([hot(k_loc == 4 + (c_loc & 15)), hot(k_halo == col_y)], axis=1)
    r, c = iota((256, 256), 0), iota((256, 256), 1)
    same_y, same_x = (r & 15) == (c & 15), (r >> 4) == (c >> 4)
    rh, ch = iota((256, 128), 0), iota((256, 128), 1)
    same_yh = (rh & 15) == (ch & 15)
    x_of = ((ch & 63) >> 3) + jnp.where((ch & 7) >= 4, 0, 8)
    same_xh = (rh >> 4) == x_of
    full, halo = [], []
    for tx, ty in zip(expand(sx, cols_x.astype(bf16)), expand(sy, cols_y.astype(bf16))):
        full.append(
            (
                jnp.where(same_y, per_x(tx[:, :256]), 0.0),
                jnp.where(same_x, per_y(ty[:, :256]), 0.0),
            )
        )
        halo.append(
            (
                jnp.where(same_yh, per_x(tx[:, 256:]), 0.0),
                jnp.where(same_xh, per_y(ty[:, 256:]), 0.0),
            )
        )
    blocks = [full[0][0], full[0][1], full[1][0] + full[1][1]]
    store_thrice(matrix, blocks)
    store_thrice(edge.at[:, : 3 * EDGE], [halo[0][0], halo[1][0], halo[0][1], halo[1][1]])


def dot_nt(a, b):
    return lax.dot_general(a, b, (((1,), (1,)), ((), ())), preferred_element_type=f32)


def react(chem, fields, rate, out, x_hi, x_lo):
    nv = out.shape[0]
    n = 16 * nv
    rows, k = iota((n, nv), 0), iota((n, nv), 1)
    pick = jnp.where(rows >> 4 == k, 1.0, 0.0).astype(bf16)
    r, c = iota((n, n), 0), iota((n, n), 1)
    same = (r & 15) == (c & 15)
    mats = []
    for part in split(chem[...] * section_step):
        t = dot_nt(dot_nt(pick, part).astype(bf16), pick)
        mats.append(jnp.where(same, t, 0.0).astype(bf16))
    for u in range(nv):
        x_hi[u], x_lo[u] = split(rate[...] * fields[u])
    for g in range(0, 16, 2):
        hi, lo = (
            jnp.concatenate(
                [x[:, 16 * q : 16 * q + 16, :].reshape(n, 128) for q in (g, g + 1)], axis=1
            )
            for x in (x_hi, x_lo)
        )
        t = mm(mats[0], hi) + mm(mats[0], lo) + mm(mats[1], hi)
        for q in range(2):
            at = 16 * (g + q)
            out[:, at : at + 16, :] = t[:, 128 * q : 128 * q + 128].reshape(nv, 16, 128)


def spread(face, lane, group):
    x = jnp.where(lane >> 3 == group, face, 0.0)
    for shift in (64, 32, 16, 8):
        x = x + pltpu.roll(x, shift, 1)
    return x


def interior(
    chem_in, fields, vel, rate_in, sx_in, sy_in, szt_in, base, edge,
    chem, sx, sy, szt, more, rate, matrix, wz, out, x_hi, x_lo, sem_in,
):
    nv = out.shape[0]
    copies = (
        (rate_in, rate),
        (chem_in, chem),
        (sx_in, sx),
        (sy_in, sy),
        (szt_in, szt),
        (vel.at[0], more.at[0]),
        (vel.at[2], more.at[1]),
    )
    ins = [pltpu.make_async_copy(src, dst, sem_in.at[k]) for k, (src, dst) in enumerate(copies)]
    for c in ins:
        c.start()
    for c in ins:
        c.wait()
    build_matrices(sx, sy, matrix, edge)
    index, n = lax.axis_index("gz"), lax.axis_size("gz")
    has_before = jnp.where(index > 0, 1.0, 0.0)
    has_after = jnp.where(index < n - 1, 1.0, 0.0)
    for f, scale in ((0, -section_step), (1, section_step)):
        hi, lo = split(szt[f, 4:132, :] * scale)
        wz[f * 128 : f * 128 + 128, 0:128] = hi
        wz[f * 128 : f * 128 + 128, 128:256] = lo
        ends = jnp.concatenate(
            [szt[f, 0:4, :] * (scale * has_before), szt[f, 132:136, :] * (scale * has_after)],
            axis=0,
        )
        hi, lo = split(jnp.concatenate([ends] * 16, axis=0))
        edge[f * 128 : f * 128 + 128, 3 * EDGE : 3 * EDGE + 128] = hi
        edge[f * 128 : f * 128 + 128, 3 * EDGE + 128 :] = lo
    react(chem, fields, rate, out, x_hi, x_lo)
    for v0 in range(0, nv, 2):
        highs, lows, zs = [], [], []
        for v in (v0, v0 + 1):
            a = fields[v]
            parts = [split(more[0] * a), split(fields[nv] * a), split(fields[nv + 1] * a)]
            highs.append(jnp.concatenate([p[0] for p in parts], axis=0))
            lows.append(jnp.concatenate([p[1] for p in parts], axis=0))
            z = split(more[1] * a)
            in_hi = jnp.concatenate([z[0], parts[2][0]], axis=1)
            in_lo = jnp.concatenate([z[1], parts[2][1]], axis=1)
            both = mm(in_hi, wz[...])
            zs.append(both[:, :128] + both[:, 128:] + mm(in_lo, wz[:, :128]))
        hi, lo = jnp.concatenate(highs, axis=1), jnp.concatenate(lows, axis=1)
        t = mm(matrix[...], jnp.concatenate([hi, lo, hi], axis=0))
        for q in range(2):
            v = v0 + q
            base[v] = (fields[v] + out[v]) + (t[:, q * 128 : q * 128 + 128] + zs[q])


def call_interior(chem, fields, vel, rate, sx, sy, szt):
    nv = fields.shape[0] - 2
    return pl.pallas_call(
        interior,
        out_shape=(
            resident(nv + 2, 256, 128),
            resident(256, 3 * EDGE + 256, dtype=bf16),
        ),
        input_output_aliases={1: 0},
        in_specs=[hbm, vm] + [hbm] * 5,
        out_specs=(vm,) * 2,
        scratch_shapes=[
            pltpu.VMEM(chem.shape, f32),
            pltpu.VMEM(sx.shape, f32),
            pltpu.VMEM(sy.shape, f32),
            pltpu.VMEM(szt.shape, f32),
            pltpu.VMEM((2, 256, 128), f32),
            pltpu.VMEM((256, 128), f32),
            pltpu.VMEM((256, 3 * WIDE), bf16),
            pltpu.VMEM((256, 256), bf16),
            pltpu.VMEM((nv, 256, 128), f32),
            pltpu.VMEM((nv, 256, 128), bf16),
            pltpu.VMEM((nv, 256, 128), bf16),
            pltpu.SemaphoreType.DMA((7,)),
        ],
        compiler_params=params(20),
        cost_estimate=cost(6 << 30, 6),
        name="interior",
    )(
        in_hbm(chem), fields, in_hbm(vel), in_hbm(rate), in_hbm(sx), in_hbm(sy), in_hbm(szt)
    )


def finish(
    base, edge, gxa, gxb, gya, gyb, gza_in, gzb_in, rows_in, final, grad,
    gza, gzb, rows, out, sem_in, sem_out,
):
    nv = out.shape[0]
    ins = [
        pltpu.make_async_copy(src, dst, sem_in.at[k])
        for k, (src, dst) in enumerate(((gza_in, gza), (gzb_in, gzb), (rows_in, rows)))
    ]
    for c in ins:
        c.start()
    for c in ins:
        c.wait()
    grad[...] = section_step * jnp.sum(rows[...], axis=0, keepdims=True)
    even = is_even("gz")
    before = jnp.where(even, gzb[...], gza[...])
    after = jnp.where(even, gza[...], gzb[...])
    low = (iota((128, 128), 1) & 4) == 0
    face = jnp.concatenate(
        [
            jnp.where(low, before, pltpu.roll(after, 4, 1)),
            jnp.where(low, pltpu.roll(before, 124, 1), after),
        ],
        axis=0,
    )
    lane = iota((256, 128), 1)
    z_hi, z_lo = split(
        jnp.concatenate([spread(face, lane, nv) * face, spread(face, lane, nv + 1) * face], axis=1)
    )
    group_of = (iota((256, 128), 0) & 127) >> 3
    tile_hi = edge[:, 3 * EDGE : 3 * EDGE + 128].astype(f32)
    tile_lo = edge[:, 3 * EDGE + 128 :].astype(f32)
    outs = []
    for v0 in range(0, nv, 2):
        highs, lows, w_his, w_los = [], [], [], []
        for v in (v0, v0 + 1):
            parts = []
            for p, q in ((gxa, gxb), (gya, gyb)):
                for f in (nv, nv + 1):
                    parts.append(split(p[v] * p[f]))
                    parts.append(split(q[v] * q[f]))
            highs.append(jnp.concatenate([p[0] for p in parts], axis=0))
            lows.append(jnp.concatenate([p[1] for p in parts], axis=0))
            w_his.append(jnp.where(group_of == v, tile_hi, 0.0).astype(bf16))
            w_los.append(jnp.where(group_of == v, tile_lo, 0.0).astype(bf16))
        hi, lo = jnp.concatenate(highs, axis=1), jnp.concatenate(lows, axis=1)
        w_hi, w_lo = jnp.concatenate(w_his, axis=1), jnp.concatenate(w_los, axis=1)
        t = mm(edge[:, : 3 * EDGE], jnp.concatenate([hi, lo, hi], axis=0))
        t = t + mm(z_hi, w_hi) + mm(z_lo, w_hi) + mm(z_hi, w_lo)
        for q in range(2):
            out[v0 + q] = base[v0 + q] + t[:, q * 128 : q * 128 + 128]
        at = slice(v0, v0 + 2)
        c = pltpu.make_async_copy(out.at[at], final.at[at], sem_out.at[v0 // 2])
        c.start()
        outs.append(c)
    for c in outs:
        c.wait()


def call_finish(base, edge, faces, rows):
    nv = base.shape[0] - 2
    return pl.pallas_call(
        finish,
        out_shape=(
            jax.ShapeDtypeStruct((nv, 256, 128), f32),
            jax.ShapeDtypeStruct((1, 128), f32),
        ),
        in_specs=[vm] * 6 + [hbm] * 3,
        out_specs=(hbm, vm),
        scratch_shapes=[
            pltpu.VMEM((128, 128), f32),
            pltpu.VMEM((128, 128), f32),
            pltpu.VMEM(rows.shape, f32),
            pltpu.VMEM((nv, 256, 128), f32),
            pltpu.SemaphoreType.DMA((3,)),
            pltpu.SemaphoreType.DMA((nv // 2,)),
        ],
        compiler_params=params(16),
        cost_estimate=cost(2 << 30, 6),
        name="finish",
    )(
        *(in_vmem(x) for x in (base, edge, *faces[:4])), *(in_hbm(x) for x in (*faces[4:], rows))
    )


def shards(
    adjoint_in,
    velocity,
    viscosity,
    rate,
    chemistry,
    stencil_x,
    stencil_y,
    stencil_z,
    sensitivity,
    patch_ids,
):
    nv = adjoint_in.shape[0]
    assert adjoint_in.shape[1:] == (16, 16, 128) and nv == 14 and sensitivity.shape[0] == 128
    devices = lax.axis_size("gx") * lax.axis_size("gy") * lax.axis_size("gz")
    adj, vel = adjoint_in.reshape(nv, 256, 128), velocity.reshape(3, 256, 128)
    gya, gyb, fields = call_pack_y(adj, vel, viscosity.reshape(256, 128))
    gya, gyb = swap(gya, gyb, "gy")
    gxa, gxb, gza, gzb, contrib = call_pack_xz(
        patch_ids, fields, vel, sensitivity, devices
    )
    gxa, gxb = swap(gxa, gxb, "gx")
    gza, gzb = swap(gza, gzb, "gz")
    rows = lax.all_to_all(contrib, AXES, 0, 0, tiled=True)
    base, edge = call_interior(
        chemistry,
        fields,
        vel,
        rate.reshape(256, 128),
        stencil_x,
        stencil_y,
        jnp.swapaxes(stencil_z, 1, 2),
    )
    faces = (gxa, gxb, gya, gyb, gza, gzb)
    out, grad = call_finish(base, edge, faces, rows)
    return out.reshape(adjoint_in.shape), grad


def solution(mesh):
    return jax.shard_map(
        shards,
        mesh=mesh,
        in_specs=(
            P(None, "gx", "gy", "gz"),
            P(None, "gx", "gy", "gz"),
            P("gx", "gy", "gz"),
            P("gx", "gy", "gz"),
            P(),
            P(),
            P(),
            P(),
            P(None, "gx", "gz"),
            P("gx", "gy", "gz"),
        ),
        out_specs=(P(None, "gx", "gy", "gz"), P(("gx", "gy", "gz"), None)),
        check_vma=False,
    )
```

```python
import functools

import jax
import jax.numpy as jnp
from jax import lax
from jax.experimental import pallas as pl
from jax.experimental.pallas import tpu as pltpu
from jax.sharding import PartitionSpec as P

section_step = 0.5
hydrogen = 5
AXES = ("gx", "gy", "gz")
f32, bf16, i32 = jnp.float32, jnp.bfloat16, jnp.int32


def swap(a, b, axis):
    n = lax.axis_size(axis)
    plan_a = [(i, i ^ 1) for i in range(n)]
    plan_b = [(i, (i - 1) % n if i % 2 == 0 else (i + 1) % n) for i in range(n)]
    return lax.ppermute(a, axis, plan_a), lax.ppermute(b, axis, plan_b)


def is_even(axis):
    return lax.rem(lax.axis_index(axis), 2) == 0


def iota(shape, dim):
    return lax.broadcasted_iota(i32, shape, dim)


def split(x):
    hi = x.astype(bf16)
    return hi, (x - hi.astype(f32)).astype(bf16)


def mm(a, b):
    return jnp.dot(a, b, preferred_element_type=f32)


hbm = pl.BlockSpec(memory_space=pl.ANY)
vm = pl.BlockSpec(memory_space=pltpu.VMEM)


def params(mib):
    return pltpu.CompilerParams(vmem_limit_bytes=mib << 20)


def cost(flops, mib):
    return pl.CostEstimate(flops=1, bytes_accessed=1024, transcendentals=0)


def in_hbm(x):
    return pltpu.with_memory_space_constraint(x, pltpu.HBM)


def in_vmem(x):
    return pltpu.with_memory_space_constraint(x, pltpu.VMEM)


def resident(*shape, dtype=f32):
    return pltpu.VMEM(shape, dtype)


CHUNKS = ((0, 4), (4, 8), (8, 12), (12, 16))


def pack_y(adj, vel, visc, gya, gyb, fields, oa, ob, sem_in, sem_out):
    nv = adj.shape[0]
    ins = []
    for k, (c0, c1) in enumerate(CHUNKS):
        top = min(c1, nv)
        group = [pltpu.make_async_copy(adj.at[c0:top], fields.at[c0:top], sem_in.at[k, 0])]
        if c1 > nv:
            group.append(pltpu.make_async_copy(vel.at[1], fields.at[nv], sem_in.at[k, 1]))
            group.append(pltpu.make_async_copy(visc, fields.at[nv + 1], sem_in.at[k, 2]))
        for c in group:
            c.start()
        ins.append(group)
    even = is_even("gy")
    outs = []
    for k, (c0, c1) in enumerate(CHUNKS):
        for c in ins[k]:
            c.wait()
        for c in range(c0, c1):
            x = fields[c].reshape(16, 16, 128)
            first = jnp.concatenate([x[8:16, 0:4, :], x[0:8, 0:4, :]], axis=1).reshape(64, 128)
            final = jnp.concatenate([x[8:16, 12:16, :], x[0:8, 12:16, :]], axis=1).reshape(64, 128)
            oa[c] = jnp.where(even, final, first)
            ob[c] = jnp.where(even, first, final)
        for side, (src, dst) in enumerate(((oa, gya), (ob, gyb))):
            c = pltpu.make_async_copy(src.at[c0:c1], dst.at[c0:c1], sem_out.at[side, k])
            c.start()
            outs.append(c)
    for c in outs:
        c.wait()


def call_pack_y(adj, vel, visc):
    nv = adj.shape[0]
    gy = pltpu.HBM((nv + 2, 64, 128), f32)
    return pl.pallas_call(
        pack_y,
        out_shape=(gy, gy, resident(nv + 2, 256, 128)),
        in_specs=[hbm] * 3,
        out_specs=(hbm, hbm, vm),
        scratch_shapes=[
            pltpu.VMEM((nv + 2, 64, 128), f32),
            pltpu.VMEM((nv + 2, 64, 128), f32),
            pltpu.SemaphoreType.DMA((4, 3)),
            pltpu.SemaphoreType.DMA((2, 4)),
        ],
        compiler_params=params(16),
        cost_estimate=cost(0, 4),
        name="pack_y",
    )(in_hbm(adj), in_hbm(vel), in_hbm(visc))


def pack_xz(
    ids, fields, vel, sens, gxa, gxb, gza, gzb, contrib,
    more, zbuf, sens_buf, sem_in, sem_x, sem_z, sem_s,
):
    channels = fields.shape[0]
    nv = channels - 2
    ins = [
        pltpu.make_async_copy(src, more.at[k], sem_in.at[k])
        for k, src in enumerate((vel.at[0], vel.at[2]))
    ]
    load_sens = pltpu.make_async_copy(sens, sens_buf, sem_s)
    for c in ins + [load_sens]:
        c.start()
    want_last = is_even("gx")
    xs = []
    for side, out in enumerate((gxa, gxb)):
        take_last = want_last if side == 0 else jnp.logical_not(want_last)
        at = pl.ds(pl.multiple_of(jnp.where(take_last, 192, 0), 64), 64)
        xs.append(pltpu.make_async_copy(fields.at[0:nv, at], out.at[0:nv], sem_x.at[side, 0]))
        xs.append(pltpu.make_async_copy(fields.at[nv + 1, at], out.at[nv + 1], sem_x.at[side, 1]))
        xs.append(pltpu.make_async_copy(more.at[0, at], out.at[nv], sem_x.at[side, 2]))
        xs[-3].start()
        xs[-2].start()
    ins[0].wait()
    xs[2].start()
    xs[5].start()
    lane = iota((256, 128), 1)
    face = jnp.zeros((256, 128), f32)
    ins[1].wait()
    for c in range(channels):
        field = more[1] if c == nv else fields[c]
        face = jnp.where(lane >> 3 == c, pltpu.roll(field, (8 * c + 4) % 128, 1), face)
    low = (iota((128, 128), 1) & 4) == 0
    top, bottom = face[:128], face[128:]
    finals = jnp.where(low, top, pltpu.roll(bottom, 4, 1))
    firsts = jnp.where(low, pltpu.roll(top, 124, 1), bottom)
    even = is_even("gz")
    zbuf[0] = jnp.where(even, finals, firsts)
    zbuf[1] = jnp.where(even, firsts, finals)
    for side, dst in enumerate((gza, gzb)):
        xs.append(pltpu.make_async_copy(zbuf.at[side], dst, sem_z.at[side]))
        xs[-1].start()
    column = jnp.sum(fields[hydrogen].reshape(16, 16, 128), axis=1)
    load_sens.wait()
    terms = jnp.sum(sens_buf[...] * column[None], axis=1)
    partial = jnp.sum(terms.T, axis=0, keepdims=True)
    owner = iota(contrib.shape, 0) == jnp.broadcast_to(ids[0], contrib.shape)
    contrib[...] = jnp.where(owner, jnp.broadcast_to(partial, contrib.shape), 0.0)
    for c in xs:
        c.wait()


def call_pack_xz(ids, fields, vel, sens, patches):
    channels = fields.shape[0]
    gx = pltpu.HBM((channels, 64, 128), f32)
    gz = pltpu.HBM((128, 128), f32)
    return pl.pallas_call(
        pack_xz,
        out_shape=(gx, gx, gz, gz, jax.ShapeDtypeStruct((patches, 128), f32)),
        in_specs=[vm, vm] + [hbm] * 2,
        out_specs=(hbm, hbm, hbm, hbm, vm),
        scratch_shapes=[
            pltpu.VMEM((2, 256, 128), f32),
            pltpu.VMEM((2, 128, 128), f32),
            pltpu.VMEM(sens.shape, f32),
            pltpu.SemaphoreType.DMA((2,)),
            pltpu.SemaphoreType.DMA((2, 3)),
            pltpu.SemaphoreType.DMA((2,)),
            pltpu.SemaphoreType.DMA,
        ],
        compiler_params=params(16),
        cost_estimate=cost(1 << 20, 6),
        name="pack_xz",
    )(ids, fields, vel, sens)


def halo_columns(axis, in_a, j, length):
    index, n = lax.axis_index(axis), lax.axis_size(axis)
    even = is_even(axis)
    after = jnp.where(even, in_a, 1 - in_a) == 1
    col = jnp.where(after, length + 4 + j, j)
    has_after = jnp.where(index < n - 1, 1, 0)
    has_before = jnp.where(index > 0, 1, 0)
    return jnp.where(jnp.where(after, has_after, has_before) == 1, col, -1)


WIDE = 3 * 256
EDGE = 4 * 128


def expand(s, cols):
    halves = [split(s[0] * -section_step), split(s[1] * section_step)]
    pieces = mm(jnp.concatenate([h for pair in halves for h in pair], axis=0), cols)
    return [pieces[32 * f : 32 * f + 16] + pieces[32 * f + 16 : 32 * f + 32] for f in range(2)]


def per_x(piece):
    shape = (16, 16, piece.shape[1])
    return jnp.broadcast_to(piece[:, None, :], shape).reshape(256, shape[2])


def per_y(piece):
    shape = (16, 16, piece.shape[1])
    return jnp.broadcast_to(piece[None], shape).reshape(256, shape[2])


def store_thrice(ref, blocks):
    wide, at = ref.shape[1] // 3, 0
    for block in blocks:
        hi, lo = split(block)
        n = block.shape[1]
        ref[:, at : at + n] = hi
        ref[:, wide + at : wide + at + n] = hi
        ref[:, 2 * wide + at : 2 * wide + at + n] = lo
        at += n


def build_matrices(sx, sy, matrix, edge):
    c_loc, k_loc = iota((24, 256), 1), iota((24, 256), 0)
    c_halo, k_halo = iota((24, 128), 1), iota((24, 128), 0)
    in_a = jnp.where(c_halo < 64, 1, 0)
    col_x = halo_columns("gx", in_a, (c_halo & 63) >> 4, 16)
    col_y = halo_columns("gy", in_a, c_halo & 3, 16)
    hot = lambda x: jnp.where(x, 1.0, 0.0)
    cols_x = jnp.concatenate([hot(k_loc == 4 + (c_loc >> 4)), hot(k_halo == col_x)], axis=1)
    cols_y = jnp.concatenate([hot(k_loc == 4 + (c_loc & 15)), hot(k_halo == col_y)], axis=1)
    r, c = iota((256, 256), 0), iota((256, 256), 1)
    same_y, same_x = (r & 15) == (c & 15), (r >> 4) == (c >> 4)
    rh, ch = iota((256, 128), 0), iota((256, 128), 1)
    same_yh = (rh & 15) == (ch & 15)
    x_of = ((ch & 63) >> 3) + jnp.where((ch & 7) >= 4, 0, 8)
    same_xh = (rh >> 4) == x_of
    full, halo = [], []
    for tx, ty in zip(expand(sx, cols_x.astype(bf16)), expand(sy, cols_y.astype(bf16))):
        full.append(
            (
                jnp.where(same_y, per_x(tx[:, :256]), 0.0),
                jnp.where(same_x, per_y(ty[:, :256]), 0.0),
            )
        )
        halo.append(
            (
                jnp.where(same_yh, per_x(tx[:, 256:]), 0.0),
                jnp.where(same_xh, per_y(ty[:, 256:]), 0.0),
            )
        )
    blocks = [full[0][0], full[0][1], full[1][0] + full[1][1]]
    store_thrice(matrix, blocks)
    store_thrice(edge.at[:, : 3 * EDGE], [halo[0][0], halo[1][0], halo[0][1], halo[1][1]])


def dot_nt(a, b):
    return lax.dot_general(a, b, (((1,), (1,)), ((), ())), preferred_element_type=f32)


def react(chem, fields, rate, out, x_hi, x_lo):
    nv = out.shape[0]
    n = 16 * nv
    rows, k = iota((n, nv), 0), iota((n, nv), 1)
    pick = jnp.where(rows >> 4 == k, 1.0, 0.0).astype(bf16)
    r, c = iota((n, n), 0), iota((n, n), 1)
    same = (r & 15) == (c & 15)
    mats = []
    for part in split(chem[...] * section_step):
        t = dot_nt(dot_nt(pick, part).astype(bf16), pick)
        mats.append(jnp.where(same, t, 0.0).astype(bf16))
    for u in range(nv):
        x_hi[u], x_lo[u] = split(rate[...] * fields[u])
    for g in range(0, 16, 2):
        hi, lo = (
            jnp.concatenate(
                [x[:, 16 * q : 16 * q + 16, :].reshape(n, 128) for q in (g, g + 1)], axis=1
            )
            for x in (x_hi, x_lo)
        )
        t = mm(mats[0], hi) + mm(mats[0], lo) + mm(mats[1], hi)
        for q in range(2):
            at = 16 * (g + q)
            out[:, at : at + 16, :] = t[:, 128 * q : 128 * q + 128].reshape(nv, 16, 128)


ARRIVE = ((12, 16), (0, 4), (4, 8), (8, 12))


def spread(face, lane, group):
    x = jnp.where(lane >> 3 == group, face, 0.0)
    for shift in (64, 32, 16, 8):
        x = x + pltpu.roll(x, shift, 1)
    return x


def interior(
    chem_in, fields, vel, rate_in, sx_in, sy_in, szt_in, base, edge,
    chem, sx, sy, szt, more, rate, matrix, wz, out, x_hi, x_lo, sem_in,
):
    nv = out.shape[0]
    copies = (
        (rate_in, rate),
        (chem_in, chem),
        (sx_in, sx),
        (sy_in, sy),
        (szt_in, szt),
        (vel.at[0], more.at[0]),
        (vel.at[2], more.at[1]),
    )
    ins = [pltpu.make_async_copy(src, dst, sem_in.at[k]) for k, (src, dst) in enumerate(copies)]
    for c in ins:
        c.start()
    ins[2].wait()
    ins[3].wait()
    build_matrices(sx, sy, matrix, edge)
    ins[4].wait()
    index, n = lax.axis_index("gz"), lax.axis_size("gz")
    has_before = jnp.where(index > 0, 1.0, 0.0)
    has_after = jnp.where(index < n - 1, 1.0, 0.0)
    for f, scale in ((0, -section_step), (1, section_step)):
        hi, lo = split(szt[f, 4:132, :] * scale)
        wz[f * 128 : f * 128 + 128, 0:128] = hi
        wz[f * 128 : f * 128 + 128, 128:256] = lo
        ends = jnp.concatenate(
            [szt[f, 0:4, :] * (scale * has_before), szt[f, 132:136, :] * (scale * has_after)],
            axis=0,
        )
        hi, lo = split(jnp.concatenate([ends] * 16, axis=0))
        edge[f * 128 : f * 128 + 128, 3 * EDGE : 3 * EDGE + 128] = hi
        edge[f * 128 : f * 128 + 128, 3 * EDGE + 128 :] = lo
    ins[0].wait()
    ins[1].wait()
    react(chem, fields, rate, out, x_hi, x_lo)
    ins[5].wait()
    ins[6].wait()
    for v0 in range(0, nv, 2):
        highs, lows, zs = [], [], []
        for v in (v0, v0 + 1):
            a = fields[v]
            parts = [split(more[0] * a), split(fields[nv] * a), split(fields[nv + 1] * a)]
            highs.append(jnp.concatenate([p[0] for p in parts], axis=0))
            lows.append(jnp.concatenate([p[1] for p in parts], axis=0))
            z = split(more[1] * a)
            in_hi = jnp.concatenate([z[0], parts[2][0]], axis=1)
            in_lo = jnp.concatenate([z[1], parts[2][1]], axis=1)
            both = mm(in_hi, wz[...])
            zs.append(both[:, :128] + both[:, 128:] + mm(in_lo, wz[:, :128]))
        hi, lo = jnp.concatenate(highs, axis=1), jnp.concatenate(lows, axis=1)
        t = mm(matrix[...], jnp.concatenate([hi, lo, hi], axis=0))
        for q in range(2):
            v = v0 + q
            base[v] = (fields[v] + out[v]) + (t[:, q * 128 : q * 128 + 128] + zs[q])


def call_interior(chem, fields, vel, rate, sx, sy, szt):
    nv = fields.shape[0] - 2
    return pl.pallas_call(
        interior,
        out_shape=(
            resident(nv + 2, 256, 128),
            resident(256, 3 * EDGE + 256, dtype=bf16),
        ),
        input_output_aliases={1: 0},
        in_specs=[hbm, vm] + [hbm] * 5,
        out_specs=(vm,) * 2,
        scratch_shapes=[
            pltpu.VMEM(chem.shape, f32),
            pltpu.VMEM(sx.shape, f32),
            pltpu.VMEM(sy.shape, f32),
            pltpu.VMEM(szt.shape, f32),
            pltpu.VMEM((2, 256, 128), f32),
            pltpu.VMEM((256, 128), f32),
            pltpu.VMEM((256, 3 * WIDE), bf16),
            pltpu.VMEM((256, 256), bf16),
            pltpu.VMEM((nv, 256, 128), f32),
            pltpu.VMEM((nv, 256, 128), bf16),
            pltpu.VMEM((nv, 256, 128), bf16),
            pltpu.SemaphoreType.DMA((7,)),
        ],
        compiler_params=params(20),
        cost_estimate=cost(6 << 30, 6),
        name="interior",
    )(
        in_hbm(chem), fields, in_hbm(vel), in_hbm(rate), in_hbm(sx), in_hbm(sy), in_hbm(szt)
    )


def finish(
    base, edge, gxa_in, gxb_in, gya_in, gyb_in, gza_in, gzb_in, rows_in, final, grad,
    gxa, gxb, gya, gyb, gza, gzb, rows, out, sem_in, sem_face, sem_out,
):
    nv = out.shape[0]
    ins = [
        pltpu.make_async_copy(src, dst, sem_in.at[k])
        for k, (src, dst) in enumerate(((gza_in, gza), (gzb_in, gzb), (rows_in, rows)))
    ]
    for c in ins:
        c.start()
    groups = []
    pairs = ((gxa_in, gxa), (gxb_in, gxb), (gya_in, gya), (gyb_in, gyb))
    for k, (c0, c1) in enumerate(ARRIVE):
        groups.append(
            [
                pltpu.make_async_copy(src.at[c0:c1], dst.at[c0:c1], sem_face.at[k, q])
                for q, (src, dst) in enumerate(pairs)
            ]
        )
        for c in groups[-1]:
            c.start()
    ins[0].wait()
    ins[1].wait()
    even = is_even("gz")
    before = jnp.where(even, gzb[...], gza[...])
    after = jnp.where(even, gza[...], gzb[...])
    low = (iota((128, 128), 1) & 4) == 0
    face = jnp.concatenate(
        [
            jnp.where(low, before, pltpu.roll(after, 4, 1)),
            jnp.where(low, pltpu.roll(before, 124, 1), after),
        ],
        axis=0,
    )
    lane = iota((256, 128), 1)
    z_hi, z_lo = split(
        jnp.concatenate([spread(face, lane, nv) * face, spread(face, lane, nv + 1) * face], axis=1)
    )
    group_of = (iota((256, 128), 0) & 127) >> 3
    tile_hi = edge[:, 3 * EDGE : 3 * EDGE + 128].astype(f32)
    tile_lo = edge[:, 3 * EDGE + 128 :].astype(f32)
    outs = []
    for v0 in (nv - 2, *range(0, nv - 2, 2)):
        for k, (c0, c1) in enumerate(ARRIVE):
            if v0 == c0:
                for c in groups[k]:
                    c.wait()
        highs, lows, w_his, w_los = [], [], [], []
        for v in (v0, v0 + 1):
            parts = []
            for p, q in ((gxa, gxb), (gya, gyb)):
                for f in (nv, nv + 1):
                    parts.append(split(p[v] * p[f]))
                    parts.append(split(q[v] * q[f]))
            highs.append(jnp.concatenate([p[0] for p in parts], axis=0))
            lows.append(jnp.concatenate([p[1] for p in parts], axis=0))
            w_his.append(jnp.where(group_of == v, tile_hi, 0.0).astype(bf16))
            w_los.append(jnp.where(group_of == v, tile_lo, 0.0).astype(bf16))
        hi, lo = jnp.concatenate(highs, axis=1), jnp.concatenate(lows, axis=1)
        w_hi, w_lo = jnp.concatenate(w_his, axis=1), jnp.concatenate(w_los, axis=1)
        t = mm(edge[:, : 3 * EDGE], jnp.concatenate([hi, lo, hi], axis=0))
        t = t + mm(z_hi, w_hi) + mm(z_lo, w_hi) + mm(z_hi, w_lo)
        for q in range(2):
            out[v0 + q] = base[v0 + q] + t[:, q * 128 : q * 128 + 128]
        at = slice(v0, v0 + 2)
        c = pltpu.make_async_copy(out.at[at], final.at[at], sem_out.at[v0 // 2])
        c.start()
        outs.append(c)
    ins[2].wait()
    grad[...] = section_step * jnp.sum(rows[...], axis=0, keepdims=True)
    for c in outs:
        c.wait()


def call_finish(base, edge, faces, rows):
    nv = base.shape[0] - 2
    return pl.pallas_call(
        finish,
        out_shape=(
            jax.ShapeDtypeStruct((nv, 256, 128), f32),
            jax.ShapeDtypeStruct((1, 128), f32),
        ),
        in_specs=[vm] * 2 + [hbm] * 7,
        out_specs=(hbm, vm),
        scratch_shapes=[
            *[pltpu.VMEM((nv + 2, 64, 128), f32)] * 4,
            pltpu.VMEM((128, 128), f32),
            pltpu.VMEM((128, 128), f32),
            pltpu.VMEM(rows.shape, f32),
            pltpu.VMEM((nv, 256, 128), f32),
            pltpu.SemaphoreType.DMA((3,)),
            pltpu.SemaphoreType.DMA((len(ARRIVE), 4)),
            pltpu.SemaphoreType.DMA((nv // 2,)),
        ],
        compiler_params=params(16),
        cost_estimate=cost(2 << 30, 6),
        name="finish",
    )(
        in_vmem(base), in_vmem(edge), *faces[:4], *(in_hbm(x) for x in (*faces[4:], rows))
    )


def shards(
    adjoint_in,
    velocity,
    viscosity,
    rate,
    chemistry,
    stencil_x,
    stencil_y,
    stencil_z,
    sensitivity,
    patch_ids,
):
    nv = adjoint_in.shape[0]
    assert adjoint_in.shape[1:] == (16, 16, 128) and nv == 14 and sensitivity.shape[0] == 128
    devices = lax.axis_size("gx") * lax.axis_size("gy") * lax.axis_size("gz")
    adj, vel = adjoint_in.reshape(nv, 256, 128), velocity.reshape(3, 256, 128)
    gya, gyb, fields = call_pack_y(adj, vel, viscosity.reshape(256, 128))
    gya, gyb = swap(gya, gyb, "gy")
    gxa, gxb, gza, gzb, contrib = call_pack_xz(
        patch_ids, fields, vel, sensitivity, devices
    )
    gxa, gxb = swap(gxa, gxb, "gx")
    gza, gzb = swap(gza, gzb, "gz")
    rows = lax.all_to_all(contrib, AXES, 0, 0, tiled=True)
    base, edge = call_interior(
        chemistry,
        fields,
        vel,
        rate.reshape(256, 128),
        stencil_x,
        stencil_y,
        jnp.swapaxes(stencil_z, 1, 2),
    )
    faces = (gxa, gxb, gya, gyb, gza, gzb)
    out, grad = call_finish(base, edge, faces, rows)
    return out.reshape(adjoint_in.shape), grad


def solution(mesh):
    return jax.shard_map(
        shards,
        mesh=mesh,
        in_specs=(
            P(None, "gx", "gy", "gz"),
            P(None, "gx", "gy", "gz"),
            P("gx", "gy", "gz"),
            P("gx", "gy", "gz"),
            P(),
            P(),
            P(),
            P(),
            P(None, "gx", "gz"),
            P("gx", "gy", "gz"),
        ),
        out_specs=(P(None, "gx", "gy", "gz"), P(("gx", "gy", "gz"), None)),
        check_vma=False,
    )
```

```python
import functools

import jax
import jax.numpy as jnp
from jax import lax
from jax.experimental import pallas as pl
from jax.experimental.pallas import tpu as pltpu
from jax.sharding import PartitionSpec as P

section_step = 0.5
hydrogen = 5
AXES = ("gx", "gy", "gz")
f32, bf16, i32 = jnp.float32, jnp.bfloat16, jnp.int32


def swap(a, b, axis):
    n = lax.axis_size(axis)
    plan_a = [(i, i ^ 1) for i in range(n)]
    plan_b = [(i, (i - 1) % n if i % 2 == 0 else (i + 1) % n) for i in range(n)]
    return lax.ppermute(a, axis, plan_a), lax.ppermute(b, axis, plan_b)


def is_even(axis):
    return lax.rem(lax.axis_index(axis), 2) == 0


def iota(shape, dim):
    return lax.broadcasted_iota(i32, shape, dim)


def split(x):
    hi = x.astype(bf16)
    return hi, (x - hi.astype(f32)).astype(bf16)


def mm(a, b):
    return jnp.dot(a, b, preferred_element_type=f32)


hbm = pl.BlockSpec(memory_space=pl.ANY)
vm = pl.BlockSpec(memory_space=pltpu.VMEM)


def params(mib):
    return pltpu.CompilerParams(vmem_limit_bytes=mib << 20)


def cost(flops, mib):
    return pl.CostEstimate(flops=1, bytes_accessed=1024, transcendentals=0)


def in_hbm(x):
    return pltpu.with_memory_space_constraint(x, pltpu.HBM)


def in_vmem(x):
    return pltpu.with_memory_space_constraint(x, pltpu.VMEM)


def resident(*shape, dtype=f32):
    return pltpu.VMEM(shape, dtype)


CHUNKS = ((0, 4), (4, 8), (8, 12), (12, 16))


def pack_y(adj, vel, visc, gya, gyb, fields, oa, ob, sem_in, sem_out):
    nv = adj.shape[0]
    ins = []
    for k, (c0, c1) in enumerate(CHUNKS):
        top = min(c1, nv)
        group = [pltpu.make_async_copy(adj.at[c0:top], fields.at[c0:top], sem_in.at[k, 0])]
        if c1 > nv:
            group.append(pltpu.make_async_copy(vel.at[1], fields.at[nv], sem_in.at[k, 1]))
            group.append(pltpu.make_async_copy(visc, fields.at[nv + 1], sem_in.at[k, 2]))
        for c in group:
            c.start()
        ins.append(group)
    even = is_even("gy")
    outs = []
    for k, (c0, c1) in enumerate(CHUNKS):
        for c in ins[k]:
            c.wait()
        for c in range(c0, c1):
            x = fields[c].reshape(16, 16, 128)
            first = jnp.concatenate([x[8:16, 0:4, :], x[0:8, 0:4, :]], axis=1).reshape(64, 128)
            final = jnp.concatenate([x[8:16, 12:16, :], x[0:8, 12:16, :]], axis=1).reshape(64, 128)
            oa[c] = jnp.where(even, final, first)
            ob[c] = jnp.where(even, first, final)
        for side, (src, dst) in enumerate(((oa, gya), (ob, gyb))):
            c = pltpu.make_async_copy(src.at[c0:c1], dst.at[c0:c1], sem_out.at[side, k])
            c.start()
            outs.append(c)
    for c in outs:
        c.wait()


def call_pack_y(adj, vel, visc):
    nv = adj.shape[0]
    gy = pltpu.HBM((nv + 2, 64, 128), f32)
    return pl.pallas_call(
        pack_y,
        out_shape=(gy, gy, resident(nv + 2, 256, 128)),
        in_specs=[hbm] * 3,
        out_specs=(hbm, hbm, vm),
        scratch_shapes=[
            pltpu.VMEM((nv + 2, 64, 128), f32),
            pltpu.VMEM((nv + 2, 64, 128), f32),
            pltpu.SemaphoreType.DMA((4, 3)),
            pltpu.SemaphoreType.DMA((2, 4)),
        ],
        compiler_params=params(16),
        cost_estimate=cost(0, 4),
        name="pack_y",
    )(in_hbm(adj), in_hbm(vel), in_hbm(visc))


def pack_xz(
    ids, fields, vel, sens, gxa, gxb, gza, gzb, contrib,
    more, zbuf, sens_buf, sem_in, sem_x, sem_z, sem_s,
):
    channels = fields.shape[0]
    nv = channels - 2
    ins = [
        pltpu.make_async_copy(src, more.at[k], sem_in.at[k])
        for k, src in enumerate((vel.at[0], vel.at[2]))
    ]
    load_sens = pltpu.make_async_copy(sens, sens_buf, sem_s)
    for c in ins + [load_sens]:
        c.start()
    want_last = is_even("gx")
    xs = []
    for side, out in enumerate((gxa, gxb)):
        take_last = want_last if side == 0 else jnp.logical_not(want_last)
        at = pl.ds(pl.multiple_of(jnp.where(take_last, 192, 0), 64), 64)
        xs.append(pltpu.make_async_copy(fields.at[0:nv, at], out.at[0:nv], sem_x.at[side, 0]))
        xs.append(pltpu.make_async_copy(fields.at[nv + 1, at], out.at[nv + 1], sem_x.at[side, 1]))
        xs.append(pltpu.make_async_copy(more.at[0, at], out.at[nv], sem_x.at[side, 2]))
        xs[-3].start()
        xs[-2].start()
    ins[0].wait()
    xs[2].start()
    xs[5].start()
    lane = iota((256, 128), 1)
    face = jnp.zeros((256, 128), f32)
    ins[1].wait()
    for c in range(channels):
        field = more[1] if c == nv else fields[c]
        face = jnp.where(lane >> 3 == c, pltpu.roll(field, (8 * c + 4) % 128, 1), face)
    low = (iota((128, 128), 1) & 4) == 0
    top, bottom = face[:128], face[128:]
    finals = jnp.where(low, top, pltpu.roll(bottom, 4, 1))
    firsts = jnp.where(low, pltpu.roll(top, 124, 1), bottom)
    even = is_even("gz")
    zbuf[0] = jnp.where(even, finals, firsts)
    zbuf[1] = jnp.where(even, firsts, finals)
    for side, dst in enumerate((gza, gzb)):
        xs.append(pltpu.make_async_copy(zbuf.at[side], dst, sem_z.at[side]))
        xs[-1].start()
    column = jnp.sum(fields[hydrogen].reshape(16, 16, 128), axis=1)
    load_sens.wait()
    terms = jnp.sum(sens_buf[...] * column[None], axis=1)
    partial = jnp.sum(terms.T, axis=0, keepdims=True)
    owner = iota(contrib.shape, 0) == jnp.broadcast_to(ids[0], contrib.shape)
    contrib[...] = jnp.where(owner, jnp.broadcast_to(partial, contrib.shape), 0.0)
    for c in xs:
        c.wait()


def call_pack_xz(ids, fields, vel, sens, patches):
    channels = fields.shape[0]
    gx = pltpu.HBM((channels, 64, 128), f32)
    gz = pltpu.HBM((128, 128), f32)
    return pl.pallas_call(
        pack_xz,
        out_shape=(gx, gx, gz, gz, jax.ShapeDtypeStruct((patches, 128), f32)),
        in_specs=[vm, vm] + [hbm] * 2,
        out_specs=(hbm, hbm, hbm, hbm, vm),
        scratch_shapes=[
            pltpu.VMEM((2, 256, 128), f32),
            pltpu.VMEM((2, 128, 128), f32),
            pltpu.VMEM(sens.shape, f32),
            pltpu.SemaphoreType.DMA((2,)),
            pltpu.SemaphoreType.DMA((2, 3)),
            pltpu.SemaphoreType.DMA((2,)),
            pltpu.SemaphoreType.DMA,
        ],
        compiler_params=params(16),
        cost_estimate=cost(1 << 20, 6),
        name="pack_xz",
    )(ids, fields, vel, sens)


def halo_columns(axis, in_a, j, length):
    index, n = lax.axis_index(axis), lax.axis_size(axis)
    even = is_even(axis)
    after = jnp.where(even, in_a, 1 - in_a) == 1
    col = jnp.where(after, length + 4 + j, j)
    has_after = jnp.where(index < n - 1, 1, 0)
    has_before = jnp.where(index > 0, 1, 0)
    return jnp.where(jnp.where(after, has_after, has_before) == 1, col, -1)


WIDE = 3 * 256
EDGE = 4 * 128


def expand(s, cols):
    halves = [split(s[0] * -section_step), split(s[1] * section_step)]
    pieces = mm(jnp.concatenate([h for pair in halves for h in pair], axis=0), cols)
    return [pieces[32 * f : 32 * f + 16] + pieces[32 * f + 16 : 32 * f + 32] for f in range(2)]


def per_x(piece):
    shape = (16, 16, piece.shape[1])
    return jnp.broadcast_to(piece[:, None, :], shape).reshape(256, shape[2])


def per_y(piece):
    shape = (16, 16, piece.shape[1])
    return jnp.broadcast_to(piece[None], shape).reshape(256, shape[2])


def store_thrice(ref, blocks):
    wide, at = ref.shape[1] // 3, 0
    for block in blocks:
        hi, lo = split(block)
        n = block.shape[1]
        ref[:, at : at + n] = hi
        ref[:, wide + at : wide + at + n] = hi
        ref[:, 2 * wide + at : 2 * wide + at + n] = lo
        at += n


def build_matrices(sx, sy, matrix, edge):
    c_loc, k_loc = iota((24, 256), 1), iota((24, 256), 0)
    c_halo, k_halo = iota((24, 128), 1), iota((24, 128), 0)
    in_a = jnp.where(c_halo < 64, 1, 0)
    col_x = halo_columns("gx", in_a, (c_halo & 63) >> 4, 16)
    col_y = halo_columns("gy", in_a, c_halo & 3, 16)
    hot = lambda x: jnp.where(x, 1.0, 0.0)
    cols_x = jnp.concatenate([hot(k_loc == 4 + (c_loc >> 4)), hot(k_halo == col_x)], axis=1)
    cols_y = jnp.concatenate([hot(k_loc == 4 + (c_loc & 15)), hot(k_halo == col_y)], axis=1)
    r, c = iota((256, 256), 0), iota((256, 256), 1)
    same_y, same_x = (r & 15) == (c & 15), (r >> 4) == (c >> 4)
    rh, ch = iota((256, 128), 0), iota((256, 128), 1)
    same_yh = (rh & 15) == (ch & 15)
    x_of = ((ch & 63) >> 3) + jnp.where((ch & 7) >= 4, 0, 8)
    same_xh = (rh >> 4) == x_of
    full, halo = [], []
    for tx, ty in zip(expand(sx, cols_x.astype(bf16)), expand(sy, cols_y.astype(bf16))):
        full.append(
            (
                jnp.where(same_y, per_x(tx[:, :256]), 0.0),
                jnp.where(same_x, per_y(ty[:, :256]), 0.0),
            )
        )
        halo.append(
            (
                jnp.where(same_yh, per_x(tx[:, 256:]), 0.0),
                jnp.where(same_xh, per_y(ty[:, 256:]), 0.0),
            )
        )
    blocks = [full[0][0], full[0][1], full[1][0] + full[1][1]]
    store_thrice(matrix, blocks)
    store_thrice(edge.at[:, : 3 * EDGE], [halo[0][0], halo[1][0], halo[0][1], halo[1][1]])


def dot_nt(a, b):
    return lax.dot_general(a, b, (((1,), (1,)), ((), ())), preferred_element_type=f32)


def react(chem, fields, rate, out, x_hi, x_lo):
    nv = out.shape[0]
    n = 16 * nv
    rows, k = iota((n, nv), 0), iota((n, nv), 1)
    pick = jnp.where(rows >> 4 == k, 1.0, 0.0).astype(bf16)
    r, c = iota((n, n), 0), iota((n, n), 1)
    same = (r & 15) == (c & 15)
    mats = []
    for part in split(chem[...] * section_step):
        t = dot_nt(dot_nt(pick, part).astype(bf16), pick)
        mats.append(jnp.where(same, t, 0.0).astype(bf16))
    for u in range(nv):
        x_hi[u], x_lo[u] = split(rate[...] * fields[u])
    for g in range(0, 16, 2):
        hi, lo = (
            jnp.concatenate(
                [x[:, 16 * q : 16 * q + 16, :].reshape(n, 128) for q in (g, g + 1)], axis=1
            )
            for x in (x_hi, x_lo)
        )
        t = mm(mats[0], hi) + mm(mats[0], lo) + mm(mats[1], hi)
        for q in range(2):
            at = 16 * (g + q)
            out[:, at : at + 16, :] = t[:, 128 * q : 128 * q + 128].reshape(nv, 16, 128)


ARRIVE = ((12, 16), (0, 4), (4, 8), (8, 12))


def spread(face, lane, group):
    x = jnp.where(lane >> 3 == group, face, 0.0)
    for shift in (64, 32, 16, 8):
        x = x + pltpu.roll(x, shift, 1)
    return x


def interior(
    chem_in, fields, vel, rate_in, sx_in, sy_in, szt_in, base, edge,
    chem, sx, sy, szt, more, rate, matrix, wz, out, x_hi, x_lo, sem_in,
):
    nv = out.shape[0]
    copies = (
        (rate_in, rate),
        (chem_in, chem),
        (sx_in, sx),
        (sy_in, sy),
        (szt_in, szt),
        (vel.at[0], more.at[0]),
        (vel.at[2], more.at[1]),
    )
    ins = [pltpu.make_async_copy(src, dst, sem_in.at[k]) for k, (src, dst) in enumerate(copies)]
    for c in ins:
        c.start()
    ins[2].wait()
    ins[3].wait()
    build_matrices(sx, sy, matrix, edge)
    ins[4].wait()
    index, n = lax.axis_index("gz"), lax.axis_size("gz")
    has_before = jnp.where(index > 0, 1.0, 0.0)
    has_after = jnp.where(index < n - 1, 1.0, 0.0)
    for f, scale in ((0, -section_step), (1, section_step)):
        hi, lo = split(szt[f, 4:132, :] * scale)
        wz[f * 128 : f * 128 + 128, 0:128] = hi
        wz[f * 128 : f * 128 + 128, 128:256] = lo
        ends = jnp.concatenate(
            [szt[f, 0:4, :] * (scale * has_before), szt[f, 132:136, :] * (scale * has_after)],
            axis=0,
        )
        hi, lo = split(jnp.concatenate([ends] * 16, axis=0))
        edge[f * 128 : f * 128 + 128, 3 * EDGE : 3 * EDGE + 128] = hi
        edge[f * 128 : f * 128 + 128, 3 * EDGE + 128 :] = lo
    ins[0].wait()
    ins[1].wait()
    react(chem, fields, rate, out, x_hi, x_lo)
    ins[5].wait()
    ins[6].wait()
    for v0 in range(0, nv, 2):
        highs, lows, zs = [], [], []
        for v in (v0, v0 + 1):
            a = fields[v]
            parts = [split(more[0] * a), split(fields[nv] * a), split(fields[nv + 1] * a)]
            highs.append(jnp.concatenate([p[0] for p in parts], axis=0))
            lows.append(jnp.concatenate([p[1] for p in parts], axis=0))
            z = split(more[1] * a)
            in_hi = jnp.concatenate([z[0], parts[2][0]], axis=1)
            in_lo = jnp.concatenate([z[1], parts[2][1]], axis=1)
            both = mm(in_hi, wz[...])
            zs.append(both[:, :128] + both[:, 128:] + mm(in_lo, wz[:, :128]))
        hi, lo = jnp.concatenate(highs, axis=1), jnp.concatenate(lows, axis=1)
        t = mm(matrix[...], jnp.concatenate([hi, lo, hi], axis=0))
        for q in range(2):
            v = v0 + q
            base[v] = (fields[v] + out[v]) + (t[:, q * 128 : q * 128 + 128] + zs[q])


def call_interior(chem, fields, vel, rate, sx, sy, szt):
    nv = fields.shape[0] - 2
    return pl.pallas_call(
        interior,
        out_shape=(
            resident(nv + 2, 256, 128),
            resident(256, 3 * EDGE + 256, dtype=bf16),
        ),
        input_output_aliases={1: 0},
        in_specs=[hbm, vm] + [hbm] * 5,
        out_specs=(vm,) * 2,
        scratch_shapes=[
            pltpu.VMEM(chem.shape, f32),
            pltpu.VMEM(sx.shape, f32),
            pltpu.VMEM(sy.shape, f32),
            pltpu.VMEM(szt.shape, f32),
            pltpu.VMEM((2, 256, 128), f32),
            pltpu.VMEM((256, 128), f32),
            pltpu.VMEM((256, 3 * WIDE), bf16),
            pltpu.VMEM((256, 256), bf16),
            pltpu.VMEM((nv, 256, 128), f32),
            pltpu.VMEM((nv, 256, 128), bf16),
            pltpu.VMEM((nv, 256, 128), bf16),
            pltpu.SemaphoreType.DMA((7,)),
        ],
        compiler_params=params(20),
        cost_estimate=pl.CostEstimate(flops=4 << 30, bytes_accessed=6 << 20, transcendentals=0),
        name="interior",
    )(
        in_hbm(chem), fields, in_hbm(vel), in_hbm(rate), in_hbm(sx), in_hbm(sy), in_hbm(szt)
    )


def finish(
    base, edge, gxa_in, gxb_in, gya_in, gyb_in, gza_in, gzb_in, rows_in, final, grad,
    gxa, gxb, gya, gyb, gza, gzb, rows, out, sem_in, sem_face, sem_out,
):
    nv = out.shape[0]
    ins = [
        pltpu.make_async_copy(src, dst, sem_in.at[k])
        for k, (src, dst) in enumerate(((gza_in, gza), (gzb_in, gzb), (rows_in, rows)))
    ]
    for c in ins:
        c.start()
    groups = []
    pairs = ((gxa_in, gxa), (gxb_in, gxb), (gya_in, gya), (gyb_in, gyb))
    for k, (c0, c1) in enumerate(ARRIVE):
        groups.append(
            [
                pltpu.make_async_copy(src.at[c0:c1], dst.at[c0:c1], sem_face.at[k, q])
                for q, (src, dst) in enumerate(pairs)
            ]
        )
        for c in groups[-1]:
            c.start()
    ins[0].wait()
    ins[1].wait()
    even = is_even("gz")
    before = jnp.where(even, gzb[...], gza[...])
    after = jnp.where(even, gza[...], gzb[...])
    low = (iota((128, 128), 1) & 4) == 0
    face = jnp.concatenate(
        [
            jnp.where(low, before, pltpu.roll(after, 4, 1)),
            jnp.where(low, pltpu.roll(before, 124, 1), after),
        ],
        axis=0,
    )
    lane = iota((256, 128), 1)
    z_hi, z_lo = split(
        jnp.concatenate([spread(face, lane, nv) * face, spread(face, lane, nv + 1) * face], axis=1)
    )
    group_of = (iota((256, 128), 0) & 127) >> 3
    tile_hi = edge[:, 3 * EDGE : 3 * EDGE + 128].astype(f32)
    tile_lo = edge[:, 3 * EDGE + 128 :].astype(f32)
    outs = []
    for v0 in (nv - 2, *range(0, nv - 2, 2)):
        for k, (c0, c1) in enumerate(ARRIVE):
            if v0 == c0:
                for c in groups[k]:
                    c.wait()
        highs, lows, w_his, w_los = [], [], [], []
        for v in (v0, v0 + 1):
            parts = []
            for p, q in ((gxa, gxb), (gya, gyb)):
                for f in (nv, nv + 1):
                    parts.append(split(p[v] * p[f]))
                    parts.append(split(q[v] * q[f]))
            highs.append(jnp.concatenate([p[0] for p in parts], axis=0))
            lows.append(jnp.concatenate([p[1] for p in parts], axis=0))
            w_his.append(jnp.where(group_of == v, tile_hi, 0.0).astype(bf16))
            w_los.append(jnp.where(group_of == v, tile_lo, 0.0).astype(bf16))
        hi, lo = jnp.concatenate(highs, axis=1), jnp.concatenate(lows, axis=1)
        w_hi, w_lo = jnp.concatenate(w_his, axis=1), jnp.concatenate(w_los, axis=1)
        t = mm(edge[:, : 3 * EDGE], jnp.concatenate([hi, lo, hi], axis=0))
        t = t + mm(z_hi, w_hi) + mm(z_lo, w_hi) + mm(z_hi, w_lo)
        for q in range(2):
            out[v0 + q] = base[v0 + q] + t[:, q * 128 : q * 128 + 128]
        at = slice(v0, v0 + 2)
        c = pltpu.make_async_copy(out.at[at], final.at[at], sem_out.at[v0 // 2])
        c.start()
        outs.append(c)
    ins[2].wait()
    grad[...] = section_step * jnp.sum(rows[...], axis=0, keepdims=True)
    for c in outs:
        c.wait()


def call_finish(base, edge, faces, rows):
    nv = base.shape[0] - 2
    return pl.pallas_call(
        finish,
        out_shape=(
            jax.ShapeDtypeStruct((nv, 256, 128), f32),
            jax.ShapeDtypeStruct((1, 128), f32),
        ),
        in_specs=[vm] * 2 + [hbm] * 7,
        out_specs=(hbm, vm),
        scratch_shapes=[
            *[pltpu.VMEM((nv + 2, 64, 128), f32)] * 4,
            pltpu.VMEM((128, 128), f32),
            pltpu.VMEM((128, 128), f32),
            pltpu.VMEM(rows.shape, f32),
            pltpu.VMEM((nv, 256, 128), f32),
            pltpu.SemaphoreType.DMA((3,)),
            pltpu.SemaphoreType.DMA((len(ARRIVE), 4)),
            pltpu.SemaphoreType.DMA((nv // 2,)),
        ],
        compiler_params=params(16),
        cost_estimate=cost(2 << 30, 6),
        name="finish",
    )(
        in_vmem(base), in_vmem(edge), *faces[:4], *(in_hbm(x) for x in (*faces[4:], rows))
    )


def shards(
    adjoint_in,
    velocity,
    viscosity,
    rate,
    chemistry,
    stencil_x,
    stencil_y,
    stencil_z,
    sensitivity,
    patch_ids,
):
    nv = adjoint_in.shape[0]
    assert adjoint_in.shape[1:] == (16, 16, 128) and nv == 14 and sensitivity.shape[0] == 128
    devices = lax.axis_size("gx") * lax.axis_size("gy") * lax.axis_size("gz")
    adj, vel = adjoint_in.reshape(nv, 256, 128), velocity.reshape(3, 256, 128)
    gya, gyb, fields = call_pack_y(adj, vel, viscosity.reshape(256, 128))
    gya, gyb = swap(gya, gyb, "gy")
    gxa, gxb, gza, gzb, contrib = call_pack_xz(
        patch_ids, fields, vel, sensitivity, devices
    )
    gxa, gxb = swap(gxa, gxb, "gx")
    gza, gzb = swap(gza, gzb, "gz")
    rows = lax.all_to_all(contrib, AXES, 0, 0, tiled=True)
    base, edge = call_interior(
        chemistry,
        fields,
        vel,
        rate.reshape(256, 128),
        stencil_x,
        stencil_y,
        jnp.swapaxes(stencil_z, 1, 2),
    )
    faces = (gxa, gxb, gya, gyb, gza, gzb)
    out, grad = call_finish(base, edge, faces, rows)
    return out.reshape(adjoint_in.shape), grad


def solution(mesh):
    return jax.shard_map(
        shards,
        mesh=mesh,
        in_specs=(
            P(None, "gx", "gy", "gz"),
            P(None, "gx", "gy", "gz"),
            P("gx", "gy", "gz"),
            P("gx", "gy", "gz"),
            P(),
            P(),
            P(),
            P(),
            P(None, "gx", "gz"),
            P("gx", "gy", "gz"),
        ),
        out_specs=(P(None, "gx", "gy", "gz"), P(("gx", "gy", "gz"), None)),
        check_vma=False,
    )
```
